32 devices in a mesh: dp: 8 (over z, y), mp: 4 (over x, core).
Axes of the slice: x: 2, y: 2, z: 4, core: 2. Of those that a mesh axis runs over, the one named last changes fastest.
Arguments:
- block_in: bfloat16 [16384, 1536], P('dp'), may hold values from -6 to 6
- cotangent: bfloat16 [16384, 1536], P('dp'), may hold values from -6 to 6
- segment_ids: int32 [32, 512], P('dp'), may hold values from 0 to 2, never falling along the last dimension, each value on 1 to 256 neighbouring positions
- w_heads: float32 [3, 1536, 3072], P(None, 'dp', 'mp'), may hold values from -0.15625 to 0.15625
- w_bc: float32 [1536, 256], P('dp', 'mp'), may hold values from -0.15625 to 0.15625
- w_dt: float32 [1536, 48], P('dp', 'mp'), may hold values from -0.15625 to 0.15625
- mom_heads: float32 [3, 1536, 3072], P(None, 'dp', 'mp'), may hold values from -160 to 160
- mom_bc: float32 [1536, 256], P('dp', 'mp'), may hold values from -160 to 160
- mom_dt: float32 [1536, 48], P('dp', 'mp'), may hold values from -160 to 160
- norm_gain: float32 [1536], replicated, may hold values from 0.5 to 1.5
- inner_params: float32 [6, 3072], P(None, 'mp'), may hold values from -0.6 to 1
- bc_params: float32 [5, 256], P(None, 'mp'), may hold values from -0.6 to 1
- head_params: float32 [3, 48], P(None, 'mp'), may hold values from -5 to 4.5
- norm_adam: float32 [2, 1536], replicated, may hold values from -11.52 to 11.52, as said below
- inner_adam: float32 [2, 6, 3072], P(None, None, 'mp'), may hold values from -11.52 to 11.52, as said below
- bc_adam: float32 [2, 5, 256], P(None, None, 'mp'), may hold values from -11.52 to 11.52, as said below
- head_adam: float32 [2, 3, 48], P(None, None, 'mp'), may hold values from -11.52 to 11.52, as said below
Outputs:
- block_out: bfloat16 [16384, 1536], P('dp')
- grad_block: float32 [16384, 1536], P('dp')
- grad_heads: float32 [3, 1536, 3072], P(None, 'dp', 'mp')
- grad_bc: float32 [1536, 256], P('dp', 'mp')
- grad_dt: float32 [1536, 48], P('dp', 'mp')
- grad_norm_gain: float32 [1536], replicated
- grad_inner: float32 [6, 3072], P(None, 'mp')
- grad_bc_params: float32 [5, 256], P(None, 'mp')
- grad_head_params: float32 [3, 48], P(None, 'mp')
- new_w_heads: float32 [3, 1536, 3072], P(None, 'dp', 'mp')
- new_w_bc: float32 [1536, 256], P('dp', 'mp')
- new_w_dt: float32 [1536, 48], P('dp', 'mp')
- new_mom_heads: float32 [3, 1536, 3072], P(None, 'dp', 'mp')
- new_mom_bc: float32 [1536, 256], P('dp', 'mp')
- new_mom_dt: float32 [1536, 48], P('dp', 'mp')
- new_norm_gain: float32 [1536], replicated
- new_inner_params: float32 [6, 3072], P(None, 'mp')
- new_bc_params: float32 [5, 256], P(None, 'mp')
- new_head_params: float32 [3, 48], P(None, 'mp')
- new_norm_adam: float32 [2, 1536], replicated
- new_inner_adam: float32 [2, 6, 3072], P(None, None, 'mp')
- new_bc_adam: float32 [2, 5, 256], P(None, None, 'mp')
- new_head_adam: float32 [2, 3, 48], P(None, None, 'mp')
The draws below stay inside these ranges and needn't reach their ends.
Inputs may be any that keep to these rules, and one draw needn't show every extreme that they name: `segment_ids`: segment numbers of one sequence never fall; a document holds at most 256 tokens. `norm_adam`: row 0 holds first moments, row 1 second moments, which are positive. `inner_adam`: row 0 holds first moments, row 1 second moments, which are positive. `bc_adam`: row 0 holds first moments, row 1 second moments, which are positive. `head_adam`: row 0 holds first moments, row 1 second moments, which are positive.
All inputs are finite; a program needn't handle non-finite values.
Results may differ from the reference program's by a relative error of at most 0.0017.
The reference program's roundings to bfloat16 on the way count: a program that leaves them out, or rounds other values in their place, can miss the bound.
Values may be sent and summed in bfloat16 or wider, within the bound.
No kernel may reach another device: no remote copies, remote signals or barrier semaphores. Data moves between devices by JAX's collectives and lax.ppermute only.
A program may use at most 256 MiB of HBM per device.

```python
import math
import jax
import jax.numpy as jnp
import numpy as np
from jax import lax

D = 1536
HEADS = 48
HEADDIM = 64
STATE = 128
CONV = 4
SPAN = 256
LEN = 512
NS_STEPS = 5
INNER = 3072
SEQS = 32
TOKENS = 16384


def draw_head_params(key, part):
    subkeys = jax.random.split(key, 3)
    log_rates = jax.random.uniform(subkeys[0], (HEADS,), jnp.float32, -3.0, 0.4)
    step_bias = jax.random.uniform(subkeys[1], (HEADS,), jnp.float32, -5.0, -3.0)
    head_ramp = jnp.arange(HEADS, dtype=jnp.float32) / max(HEADS - 1, 1)
    skip_gain = jax.random.uniform(subkeys[2], (HEADS,), jnp.float32, 0.5, 1.5) * (1.0 + 2.0 * head_ramp)
    return jnp.stack([log_rates, step_bias, skip_gain])


def adam_pair(key, shape):
    grad_scale = 0.3 * TOKENS ** 0.5
    subkeys = jax.random.split(key, 2)
    moment_one = 0.1 * grad_scale * jax.random.truncated_normal(subkeys[0], -3.0, 3.0, shape, jnp.float32)
    moment_two = 0.001 * grad_scale * grad_scale * jax.random.uniform(subkeys[1], shape, jnp.float32, 0.5, 1.5)
    return jnp.stack([moment_one, moment_two])


def draw_norm_adam(key, part):
    return adam_pair(key, (D,))


def draw_inner_adam(key, part):
    return adam_pair(key, (CONV + 2, INNER))


def draw_bc_adam(key, part):
    return adam_pair(key, (CONV + 1, 2 * STATE))


def draw_head_adam(key, part):
    return adam_pair(key, (3, HEADS))


def spiked(drawn, own_key, source, target, blocks, factor):
    owner, partner = [(jnp.arange(drawn.shape[axis_at]) // (drawn.shape[axis_at] // blocks)).reshape([-1 if axis == axis_at else 1 for axis in range(drawn.ndim)]) for axis_at in (source, target)]
    chosen = jax.random.permutation(own_key, blocks)[partner]
    strong = (owner == chosen) | (owner == (partner + blocks // 2) % blocks)
    return jnp.where(strong, factor * drawn, drawn)


def block_levels(own_key, dims, shards, least, high):
    gain, own = 1.0, jax.random.fold_in(own_key, 6)
    for position, parts in shards:
        heights = jnp.exp(jax.random.uniform(jax.random.fold_in(own, position), (parts,), jnp.float32, least / len(shards), high / len(shards)))
        gain = gain * jnp.repeat(heights, dims[position] // parts).reshape([-1 if axis == position else 1 for axis in range(len(dims))])
    return gain


def profile(count, total, limit, slope):
    loads = [(1 << 20) // math.isqrt(rank ** slope) + 1 for rank in range(2, count + 1)]
    rest, holding = total - limit - (count - 1), [1] * (count - 1)
    while rest > 0:
        candidates = [i for i in range(count - 1) if holding[i] < limit]
        mass, left = sum([loads[i] for i in candidates]), rest
        for i in candidates:
            more = min(limit - holding[i], max(1, left * loads[i] // mass), rest)
            holding[i] = holding[i] + more
            rest = rest - more
    return np.array([limit] + holding)


def uneven_parts(own_key, number_of, total, limit, lean):
    if number_of == 2:
        one = jax.random.randint(own_key, (), max(1, total - limit), min(limit, total - 1) + 1)
        return jnp.stack([one, total - one])
    tallies = jnp.asarray(profile(number_of, total, limit, lean), jnp.int32)
    couples = (number_of - 1) // 2
    giver, taker = tallies[1:1 + 2 * couples:2], tallies[2:2 + 2 * couples:2]
    room = jnp.minimum(giver - 1, limit - taker)
    passed = jax.random.randint(jax.random.fold_in(own_key, 1), (couples,), 0, 1 << 20) % (room + 1)
    tallies = tallies.at[1:1 + 2 * couples:2].set(giver - passed).at[2:2 + 2 * couples:2].set(taker + passed)
    return tallies[jax.random.permutation(jax.random.fold_in(own_key, 2), number_of)]


def centred(rng, dims, width, limit, cuts=(), kind=jnp.bfloat16):
    array = width * jax.random.normal(rng, dims, jnp.float32)
    if cuts:
        array = array * block_levels(rng, dims, cuts, -0.22, 0.18)
    return jnp.clip(array, -limit, limit).astype(kind)


def heavy_noise(key, extent, width, bound, cuts, heavy, kind=jnp.bfloat16):
    drawn = width * jax.random.normal(key, extent, jnp.float32)
    if cuts:
        drawn = drawn * block_levels(key, extent, cuts, -0.22, 0.18)
    return jnp.clip(spiked(drawn, jax.random.fold_in(key, 3), *heavy), -bound, bound).astype(kind)


def setup_inputs(seed: int = 0) -> dict:
    key_list = jax.random.split(jax.random.key(seed), 18)
    block_in = heavy_noise(key_list[0], (TOKENS, D), 1.0, 6.0, ((0, 8),), (0, 1, 8, 2.0))
    cotangent = heavy_noise(key_list[1], (TOKENS, D), 1.0, 6.0, ((0, 8),), (0, 1, 8, 2.0))
    segment_ids = jax.vmap(lambda own: jnp.searchsorted(jnp.cumsum(uneven_parts(own, 3, LEN, LEN // 2, 0)), jnp.arange(LEN), side="right"))(jax.random.split(key_list[2], SEQS)).reshape((SEQS, LEN)).astype(jnp.int32)
    w_heads = centred(key_list[3], (3, D, INNER), D ** -0.5, 0.15625, ((1, 8), (2, 4)), jnp.float32)
    w_bc = centred(key_list[4], (D, 2 * STATE), D ** -0.5, 0.15625, ((0, 8), (1, 4)), jnp.float32)
    w_dt = centred(key_list[5], (D, HEADS), D ** -0.5, 0.15625, ((0, 8), (1, 4)), jnp.float32)
    mom_heads = centred(key_list[6], (3, D, INNER), (0.2 * TOKENS ** 0.5), 160.0, ((1, 8), (2, 4)), jnp.float32)
    mom_bc = centred(key_list[7], (D, 2 * STATE), (0.2 * TOKENS ** 0.5), 160.0, ((0, 8), (1, 4)), jnp.float32)
    mom_dt = centred(key_list[8], (D, HEADS), (0.2 * TOKENS ** 0.5), 160.0, ((0, 8), (1, 4)), jnp.float32)
    norm_gain = jnp.clip(1.0 + 0.1 * jax.random.normal(key_list[9], (D,), jnp.float32), 0.5, 1.5)
    inner_params = jnp.clip(-0.6 + 1.6 * jax.random.uniform(key_list[10], (CONV + 2, INNER), jnp.float32) ** block_levels(key_list[10], (CONV + 2, INNER), ((1, 4),), -0.2, 0.2), -0.6, 1.0)
    bc_params = jnp.clip(-0.6 + 1.6 * jax.random.uniform(key_list[11], (CONV + 1, 2 * STATE), jnp.float32) ** block_levels(key_list[11], (CONV + 1, 2 * STATE), ((1, 4),), -0.2, 0.2), -0.6, 1.0)
    head_params = draw_head_params(jax.random.fold_in(key_list[17], 71), 0)
    norm_adam = draw_norm_adam(jax.random.fold_in(key_list[17], 71), 0)
    inner_adam = draw_inner_adam(jax.random.fold_in(key_list[17], 71), 0)
    bc_adam = draw_bc_adam(jax.random.fold_in(key_list[17], 71), 0)
    head_adam = draw_head_adam(jax.random.fold_in(key_list[17], 71), 0)
    return {"block_in": block_in, "cotangent": cotangent, "segment_ids": segment_ids, "w_heads": w_heads, "w_bc": w_bc, "w_dt": w_dt, "mom_heads": mom_heads, "mom_bc": mom_bc, "mom_dt": mom_dt, "norm_gain": norm_gain, "inner_params": inner_params, "bc_params": bc_params, "head_params": head_params, "norm_adam": norm_adam, "inner_adam": inner_adam, "bc_adam": bc_adam, "head_adam": head_adam}


highest = lax.Precision.HIGHEST
eps_norm = 1e-05
ns_coeffs = (3.4445, -4.775, 2.0315)
momentum_beta = 0.95
muon_rate = 0.02
decay_rate = 0.1
adam_rate = 0.1
adam_first = 0.9
adam_second = 0.999
adam_steps = 2.0

def causal_conv(values, conv_par, segments):
    result = conv_par[CONV] + conv_par[CONV - 1] * values
    for offset in range(1, CONV):
        shifted = jnp.pad(values[:, :-offset], ((0, 0), (offset, 0), (0, 0)))
        earlier = jnp.pad(segments[:, :-offset], ((0, 0), (offset, 0)), constant_values=-1)
        linked = (earlier == segments)[:, :, None]
        result = result + conv_par[CONV - 1 - offset] * jnp.where(linked, shifted, 0.0)
    return result

def convolve_state(raw_vals, conv_par, segments):
    return jax.nn.silu(causal_conv(raw_vals, conv_par, segments))

def mixer(x_raw, gate_z, step_raw, state_vals, conv_par, head_par, segments):
    x_conv = jax.nn.silu(causal_conv(x_raw[None], conv_par, segments[None])[0])
    length = x_raw.shape[0]
    head_count = step_raw.shape[1]
    head_width = x_raw.shape[1] // head_count
    state_size = state_vals.shape[1] // 2
    blocks = length // SPAN
    step_size = jax.nn.softplus(step_raw + head_par[1])
    log_decay = -jnp.exp(head_par[0]) * step_size
    x_heads = x_conv.reshape(blocks, SPAN, head_count, head_width)
    inputs = x_heads * step_size.reshape(blocks, SPAN, head_count, 1)
    b_mat = state_vals[:, :state_size].reshape(blocks, SPAN, state_size)
    c_mat = state_vals[:, state_size:].reshape(blocks, SPAN, state_size)
    seg_blocks = segments.reshape(blocks, SPAN)
    cumul = jnp.cumsum(log_decay.reshape(blocks, SPAN, head_count), axis=1)
    cum_heads = jnp.swapaxes(cumul, 1, 2)
    scores = jnp.einsum('ctn,csn->cts', c_mat, b_mat, precision=highest)
    positions = jnp.arange(SPAN)
    allowed = (positions[:, None] >= positions[None, :]) & (seg_blocks[:, :, None] == seg_blocks[:, None, :])
    gaps = cum_heads[:, :, :, None] - cum_heads[:, :, None, :]
    weights = jnp.exp(jnp.where(allowed[:, None], gaps, -jnp.inf)) * scores[:, None]
    inner_out = jnp.einsum('chts,cshp->cthp', weights, inputs, precision=highest)
    span_total = cumul[:, SPAN - 1, :]
    tail_ok = seg_blocks == seg_blocks[:, SPAN - 1:]
    tail_decay = jnp.exp(jnp.where(tail_ok[:, :, None], span_total[:, None, :] - cumul, -jnp.inf))
    states = jnp.einsum('cshp,csn->chpn', inputs * tail_decay[..., None], b_mat, precision=highest)
    carried = jnp.zeros((head_count, head_width, state_size), jnp.float32)
    prev_end = jnp.full((), -1, segments.dtype)
    carried_out = []
    for block_idx in range(blocks):
        entry_ok = seg_blocks[block_idx] == prev_end
        head_decay = jnp.exp(cumul[block_idx])
        contrib = jnp.einsum('tn,hpn->thp', c_mat[block_idx], carried, precision=highest) * head_decay[:, :, None]
        carried_out.append(jnp.where(entry_ok[:, None, None], contrib, 0.0))
        keep_state = seg_blocks[block_idx, SPAN - 1] == prev_end
        carried = jnp.where(keep_state, jnp.exp(span_total[block_idx])[:, None, None] * carried, 0.0) + states[block_idx]
        prev_end = seg_blocks[block_idx, SPAN - 1]
    mixed_heads = inner_out + jnp.stack(carried_out) + head_par[2][:, None] * x_heads
    return mixed_heads.reshape(length, head_count * head_width) * jax.nn.silu(gate_z)

def run_mixer(x_raw, gate_z, step_raw, state_vals, conv_par, head_par, segments):
    seq_here, length = segments.shape

    def per_sequence(item):
        return mixer(item[0], item[1], item[2], item[3], conv_par, head_par, item[4])
    stacked = lax.map(per_sequence, (x_raw.reshape(seq_here, length, -1), gate_z.reshape(seq_here, length, -1), step_raw.reshape(seq_here, length, -1), state_vals.reshape(seq_here, length, -1), segments))
    return stacked.reshape(seq_here * length, -1)

def run_mixer_back(x_raw, gate_z, step_raw, state_vals, conv_par, head_par, segments, d_mixed):
    seq_here, length = segments.shape

    def per_sequence(item):

        def local_fn(a, b, c, d, e, f):
            return mixer(a, b, c, d, e, f, item[4])
        primal, back_fn = jax.vjp(local_fn, item[0], item[1], item[2], item[3], conv_par, head_par)
        return back_fn(item[5])
    grads = lax.map(per_sequence, (x_raw.reshape(seq_here, length, -1), gate_z.reshape(seq_here, length, -1), step_raw.reshape(seq_here, length, -1), state_vals.reshape(seq_here, length, -1), segments, d_mixed.reshape(seq_here, length, -1)))
    tok_rows = seq_here * length
    return (grads[0].reshape(tok_rows, -1), grads[1].reshape(tok_rows, -1), grads[2].reshape(tok_rows, -1), grads[3].reshape(tok_rows, -1), lax.optimization_barrier(jnp.sum(grads[4], axis=0)), lax.optimization_barrier(jnp.sum(grads[5], axis=0)))

def gated_norm(mixed, squares, gain_row):
    return mixed * lax.rsqrt(squares / INNER + eps_norm)[:, None] * gain_row

def input_norm(features, gain_row):
    return features * lax.rsqrt(lax.optimization_barrier(jnp.mean(features * features, axis=1, keepdims=True)) + eps_norm) * gain_row

def orthogonalize(blocks_in):
    frob_norm = jnp.sqrt(lax.optimization_barrier(jnp.sum(blocks_in * blocks_in, axis=(1, 2), keepdims=True)))
    current = blocks_in / (frob_norm + 1e-07)
    for sweep_idx in range(NS_STEPS):
        gram_mat = jnp.einsum('kdp,kdq->kpq', current, current, precision=highest)
        poly_mat = ns_coeffs[1] * gram_mat + ns_coeffs[2] * jnp.einsum('kpq,kqr->kpr', gram_mat, gram_mat, precision=highest)
        current = ns_coeffs[0] * current + jnp.einsum('kdp,kpq->kdq', current, poly_mat, precision=highest)
    return current

def adam_update(params_in, gradient, state_pair):
    moment_one = adam_first * state_pair[0] + (1.0 - adam_first) * gradient
    moment_two = adam_second * state_pair[1] + (1.0 - adam_second) * gradient * gradient
    scaled = moment_one / (1.0 - adam_first ** adam_steps) / (jnp.sqrt(moment_two / (1.0 - adam_second ** adam_steps)) + 1e-08)
    return (params_in - adam_rate * scaled, jnp.stack([moment_one, moment_two]))

def muon_update(weight_vals, ortho_vals):
    return weight_vals - muon_rate * (0.2 * math.sqrt(D) * ortho_vals + decay_rate * weight_vals)

def reference(block_in, cotangent, segment_ids, w_heads, w_bc, w_dt, mom_heads, mom_bc, mom_dt, norm_gain, inner_params, bc_params, head_params, norm_adam, inner_adam, bc_adam, head_adam):
    w_zed = w_heads[0].astype(jnp.bfloat16)
    w_xin = w_heads[1].astype(jnp.bfloat16)
    w_out = w_heads[2].astype(jnp.bfloat16)
    w_state = w_bc.astype(jnp.bfloat16)
    w_step = w_dt.astype(jnp.bfloat16)
    group = math.gcd(SEQS, max(1, 4096 // LEN))
    count = SEQS // group
    tok_rows = group * LEN
    conv_inner = inner_params[:CONV + 1]
    gate_gain = inner_params[CONV + 1]
    x_blocks = block_in.reshape(count, tok_rows, D)
    g_blocks = cotangent.reshape(count, tok_rows, D)
    seg_all = segment_ids.reshape(count, group, LEN)

    def block_step(totals, item):
        x_block, g_block, seg_block = item
        x_float = x_block.astype(jnp.float32)
        normed = input_norm(x_float, norm_gain).astype(jnp.bfloat16)
        gate_z = jnp.dot(normed, w_zed, preferred_element_type=jnp.float32)
        x_raw = jnp.dot(normed, w_xin, preferred_element_type=jnp.float32)
        state_raw = jnp.dot(normed, w_state, preferred_element_type=jnp.float32).reshape(group, LEN, 2 * STATE)
        step_raw = jnp.dot(normed, w_step, preferred_element_type=jnp.float32)
        state_act = convolve_state(state_raw, bc_params, seg_block).astype(jnp.bfloat16)
        state_vals = lax.optimization_barrier(state_act).astype(jnp.float32).reshape(tok_rows, 2 * STATE)
        mixed = run_mixer(x_raw, gate_z, step_raw, state_vals, conv_inner, head_params, seg_block)
        squares = lax.optimization_barrier(jnp.sum(mixed * mixed, axis=1))
        out_bf = gated_norm(mixed, squares, gate_gain).astype(jnp.bfloat16)
        branch_out = jnp.einsum('rc,dc->rd', out_bf, w_out, preferred_element_type=jnp.float32)
        y_block = (x_float + branch_out).astype(jnp.bfloat16)
        back_out = jnp.einsum('rd,dc->rc', g_block, w_out, preferred_element_type=jnp.float32)
        grad_wout = jnp.einsum('rd,rc->dc', g_block, out_bf, preferred_element_type=jnp.float32)
        primal, gate_back = jax.vjp(gated_norm, mixed, squares, gate_gain)
        back_mixed, back_squares, back_gain = gate_back(back_out)
        back_mixed = back_mixed + 2.0 * mixed * back_squares[:, None]
        back_xraw, back_gate, back_step, back_state, back_conv, back_head = run_mixer_back(x_raw, gate_z, step_raw, state_vals, conv_inner, head_params, seg_block, back_mixed)

        def state_fn(raw_vals, conv_par):
            return convolve_state(raw_vals, conv_par, seg_block)
        primal, state_back = jax.vjp(state_fn, state_raw, bc_params)
        back_sraw, back_bcpar = state_back(back_state.reshape(group, LEN, 2 * STATE))
        gate_bf = back_gate.astype(jnp.bfloat16)
        xraw_bf = back_xraw.astype(jnp.bfloat16)
        sraw_bf = back_sraw.reshape(tok_rows, 2 * STATE).astype(jnp.bfloat16)
        step_bf = back_step.astype(jnp.bfloat16)
        back_normed = jnp.einsum('rc,dc->rd', gate_bf, w_zed, preferred_element_type=jnp.float32)
        back_normed = back_normed + jnp.einsum('rc,dc->rd', xraw_bf, w_xin, preferred_element_type=jnp.float32)
        back_normed = back_normed + jnp.einsum('rc,dc->rd', sraw_bf, w_state, preferred_element_type=jnp.float32)
        back_normed = back_normed + jnp.einsum('rc,dc->rd', step_bf, w_step, preferred_element_type=jnp.float32)
        grad_zed = jnp.einsum('rd,rc->dc', normed, gate_bf, preferred_element_type=jnp.float32)
        grad_xin = jnp.einsum('rd,rc->dc', normed, xraw_bf, preferred_element_type=jnp.float32)
        grad_state = jnp.einsum('rd,rc->dc', normed, sraw_bf, preferred_element_type=jnp.float32)
        grad_step = jnp.einsum('rd,rc->dc', normed, step_bf, preferred_element_type=jnp.float32)
        primal, norm_back = jax.vjp(input_norm, x_float, norm_gain)
        back_x, back_ngain = norm_back(back_normed)
        dx_block = g_block.astype(jnp.float32) + back_x
        updates = (grad_zed, grad_xin, grad_wout, grad_state, grad_step, back_ngain, back_conv, back_gain, back_bcpar, back_head)
        new_totals = tuple((total_now + update_now for total_now, update_now in zip(totals, updates)))
        return (new_totals, (y_block, dx_block))
    start_totals = (jnp.zeros((D, INNER), jnp.float32), jnp.zeros((D, INNER), jnp.float32), jnp.zeros((D, INNER), jnp.float32), jnp.zeros((D, 2 * STATE), jnp.float32), jnp.zeros((D, HEADS), jnp.float32), jnp.zeros((D,), jnp.float32), jnp.zeros((CONV + 1, INNER), jnp.float32), jnp.zeros((INNER,), jnp.float32), jnp.zeros((CONV + 1, 2 * STATE), jnp.float32), jnp.zeros((3, HEADS), jnp.float32))
    totals, outputs = lax.scan(block_step, start_totals, (x_blocks, g_blocks, seg_all))
    block_out = outputs[0].reshape(TOKENS, D)
    grad_block = outputs[1].reshape(TOKENS, D)
    grad_heads = jnp.stack([totals[0], totals[1], totals[2]])
    grad_bc = totals[3]
    grad_dt = totals[4]
    grad_norm_gain = totals[5]
    grad_inner = jnp.concatenate([totals[6], totals[7][None]], axis=0)
    grad_bc_params = totals[8]
    grad_head_params = totals[9]
    new_mom_heads = momentum_beta * mom_heads + grad_heads
    new_mom_bc = momentum_beta * mom_bc + grad_bc
    new_mom_dt = momentum_beta * mom_dt + grad_dt
    head_blocks = new_mom_heads.reshape(3, D, HEADS, HEADDIM).transpose(0, 2, 1, 3).reshape(3 * HEADS, D, HEADDIM)
    ortho = orthogonalize(head_blocks)
    ortho_heads = ortho.reshape(3, HEADS, D, HEADDIM).transpose(0, 2, 1, 3).reshape(3, D, INNER)
    small_blocks = jnp.stack([new_mom_bc[:, :STATE], new_mom_bc[:, STATE:], jnp.pad(new_mom_dt, ((0, 0), (0, STATE - HEADS)))])
    ortho_small = orthogonalize(small_blocks)
    ortho_state = jnp.concatenate([ortho_small[0], ortho_small[1]], axis=1)
    ortho_step = ortho_small[2][:, :HEADS]
    new_w_heads = muon_update(w_heads, ortho_heads)
    new_w_bc = muon_update(w_bc, ortho_state)
    new_w_dt = muon_update(w_dt, ortho_step)
    new_norm_gain, new_norm_adam = adam_update(norm_gain, grad_norm_gain, norm_adam)
    new_inner_params, new_inner_adam = adam_update(inner_params, grad_inner, inner_adam)
    new_bc_params, new_bc_adam = adam_update(bc_params, grad_bc_params, bc_adam)
    new_head_params, new_head_adam = adam_update(head_params, grad_head_params, head_adam)
    return (block_out, grad_block, grad_heads, grad_bc, grad_dt, grad_norm_gain, grad_inner, grad_bc_params, grad_head_params, new_w_heads, new_w_bc, new_w_dt, new_mom_heads, new_mom_bc, new_mom_dt, new_norm_gain, new_inner_params, new_bc_params, new_head_params, new_norm_adam, new_inner_adam, new_bc_adam, new_head_adam)
```

```python
import functools
import math

import jax
import jax.numpy as jnp
from jax import lax
from jax.experimental import pallas as pl
from jax.experimental.pallas import tpu as pltpu
from jax.sharding import PartitionSpec as P


D = 1536
CONV = 4
NS_STEPS = 5
INNER = 3072

eps_norm = 1e-05
ns_coeffs = (3.4445, -4.775, 2.0315)
momentum_beta = 0.95
muon_rate = 0.02
decay_rate = 0.1
adam_rate = 0.1
adam_first = 0.9
adam_second = 0.999
adam_steps = 2.0

f32 = jnp.float32
bf16 = jnp.bfloat16
HEADDIM = 64
STATE = 128
SPAN = 256
TILE = 128

NN = (((1,), (0,)), ((), ()))
NT = (((1,), (1,)), ((), ()))
TN = (((0,), (0,)), ((), ()))


def dot(lhs, rhs, dims=NN):
    return lax.dot_general(lhs, rhs, dims, preferred_element_type=f32)


def split(value):
    high = value.astype(bf16)
    return high, (value - high.astype(f32)).astype(bf16)


def sigmoid(value):
    return 0.5 + 0.5 * jnp.tanh(0.5 * value)


def shift_right(value, amount):
    return pltpu.roll(value, amount, axis=1)


def shift_left(value, amount):
    return pltpu.roll(value, value.shape[1] - amount, axis=1)


def lane_iota(shape):
    return lax.broadcasted_iota(jnp.int32, shape, len(shape) - 1)


def conv_masks(seg):
    at = lane_iota(seg.shape)
    return [
        jnp.where((shift_right(seg, k) == seg) & (at >= k), 1.0, 0.0).astype(f32)[:1]
        for k in (1, 2, 3)
    ]


def segment_scan(value, seg, reach):
    at = lane_iota(value.shape)
    step = 1
    while step < reach:
        linked = (shift_right(seg, step) == seg) & (at >= step)
        value = value + jnp.where(linked, shift_right(value, step), 0.0)
        step *= 2
    return value


def segment_scan_back(value, seg, reach):
    length = value.shape[1]
    at = lane_iota(value.shape)
    step = 1
    while step < reach:
        linked = (shift_left(seg, step) == seg) & (at < length - step)
        value = value + jnp.where(linked, shift_left(value, step), 0.0)
        step *= 2
    return value


def head_rows(step_raw, seg, headcol):
    biased = step_raw + headcol[:, 1:2]
    dt = jnp.maximum(biased, 0.0) + jnp.log1p(jnp.exp(-jnp.abs(biased)))
    rate = -jnp.exp(headcol[:, 0:1])
    cum = segment_scan(rate * dt, seg, SPAN)
    last_cum = cum[:, SPAN - 1 : SPAN]
    last_seg = seg[:, SPAN - 1 : SPAN]
    same = seg == last_seg
    at = lane_iota(cum.shape)
    tail = jnp.exp(jnp.where(same & (at < SPAN), last_cum - cum, -1e30))
    head = jnp.exp(jnp.where(same & (at >= SPAN), cum - last_cum, -1e30))
    return biased, dt, rate, cum, tail, head


def decay_tile(cum_row, cum_col, s0, t0):
    gap = cum_row[:, t0 : t0 + TILE] - cum_col[s0 // TILE]
    return jnp.exp(jnp.minimum(gap, 0.0))


def tiles_of(block):
    base = block * SPAN
    return ((base, base), (base, base + TILE), (base + TILE, base + TILE))


def score_tiles(bc, seg, seg_col, score_ref):
    row = lax.broadcasted_iota(jnp.int32, (TILE, TILE), 0)
    col = lax.broadcasted_iota(jnp.int32, (TILE, TILE), 1)
    for block in range(2):
        base = block * SPAN
        full = dot(bc[:STATE, base : base + SPAN], bc[STATE:, base : base + SPAN], TN)
        for index, (s0, t0) in enumerate(tiles_of(block)):
            part = full[s0 - base : s0 - base + TILE, t0 - base : t0 - base + TILE]
            ok = seg_col[s0 // TILE] == seg[:1, t0 : t0 + TILE]
            if s0 == t0:
                ok = ok & (row <= col)
            score_ref[block * 3 + index] = jnp.where(ok, part, 0.0)


def column_of(row8):
    return [
        jnp.broadcast_to(row8[:1, s0 : s0 + TILE], (TILE, TILE)).T
        for s0 in range(0, row8.shape[1], TILE)
    ]


def conv_of(raw, taps, masks):
    shifted = [shift_right(raw, k + 1) * masks[k] for k in range(3)]
    pre = taps[4] + taps[3] * raw + taps[2] * shifted[0] + taps[1] * shifted[1] + taps[0] * shifted[2]
    return pre, shifted


def square_of(tiles):
    zero = jnp.zeros_like(tiles[0])
    return jnp.concatenate(
        [jnp.concatenate([tiles[0], tiles[1]], axis=1), jnp.concatenate([zero, tiles[2]], axis=1)],
        axis=0,
    )


def forward_kernel(heads, raw_ref, step_ref, bc_ref, seg_ref, taps_ref, headcol_ref, skip_ref,
                   y_ref, state_ref, score_ref, rows_ref):
    length = raw_ref.shape[1]
    seg = jnp.broadcast_to(seg_ref[0], (8, length))
    bc = bc_ref[...]
    seg_col = column_of(seg.astype(f32))
    score_tiles(bc, seg.astype(f32), seg_col, score_ref)
    masks = conv_masks(seg)
    seg16 = jnp.broadcast_to(seg_ref[0], (step_ref.shape[0], length))
    _, dt, _, cum, tail, head = head_rows(step_ref[...], seg16, headcol_ref[...])
    rows_ref[0] = dt
    rows_ref[1] = cum
    rows_ref[2] = tail
    rows_ref[3] = head

    def per_head(h, carry):
        rows = pl.ds(pl.multiple_of(h * HEADDIM, HEADDIM), HEADDIM)
        raw = raw_ref[rows, :]
        taps_all = taps_ref[rows, :]
        taps = [taps_all[:, k : k + 1] for k in range(5)]
        pre, _ = conv_of(raw, taps, masks)
        xc = pre * sigmoid(pre)
        dt_row = rows_ref[0, pl.ds(h, 1), :]
        cum_row = rows_ref[1, pl.ds(h, 1), :]
        xbar = xc * dt_row
        xh, xl = split(xbar)
        cum_col = column_of(jnp.broadcast_to(cum_row, (8, length)))
        parts = []
        for block in range(2):
            base = block * SPAN
            tiles = [
                decay_tile(cum_row, cum_col, s0, t0) * score_ref[block * 3 + i]
                for i, (s0, t0) in enumerate(tiles_of(block))
            ]
            halves = [split(tile) for tile in tiles]
            wh = square_of([p[0] for p in halves])
            wl = square_of([p[1] for p in halves])
            bxh, bxl = xh[:, base : base + SPAN], xl[:, base : base + SPAN]
            both = dot(jnp.concatenate([bxh, bxl], axis=0), wh)
            parts.append(both[:HEADDIM] + both[HEADDIM:] + dot(bxh, wl))
        tail_row = rows_ref[2, pl.ds(h, 1), :]
        head_row = rows_ref[3, pl.ds(h, 1), :]
        th, tl = split(xbar[:, :SPAN] * tail_row[:, :SPAN])
        both = dot(jnp.concatenate([th, tl], axis=0), bc[:STATE, :SPAN], NT)
        state = both[:HEADDIM] + both[HEADDIM:]
        state_ref[0, rows, :] = state
        sh, sl = split(state)
        both = dot(jnp.concatenate([sh, sl], axis=0), bc[STATE:, SPAN:])
        cross = (both[:HEADDIM] + both[HEADDIM:]) * head_row[:, SPAN:]
        skip = skip_ref[2, h]
        y_ref[rows, :SPAN] = parts[0] + skip * xc[:, :SPAN]
        y_ref[rows, SPAN:] = parts[1] + cross + skip * xc[:, SPAN:]
        return carry

    lax.fori_loop(0, heads, per_head, 0, unroll=4)


def backward_kernel(first_head, heads, raw_ref, z_ref, y_ref, do_ref, step_ref, bc_ref, seg_ref, norm_ref,
                    state_ref, taps_ref, headcol_ref, skip_ref,
                    dzx_ref, dstep_ref, dbc_ref, gsum_ref, ghead_ref,
                    score_ref, rows_ref, dscore_ref, sums_ref, dcross_ref, gconv_ref):
    item = pl.program_id(0)
    length = raw_ref.shape[1]
    seg = jnp.broadcast_to(seg_ref[0], (8, length))
    bc = bc_ref[...]
    seg_col = column_of(seg.astype(f32))
    score_tiles(bc, seg.astype(f32), seg_col, score_ref)
    masks = conv_masks(seg)
    seg16 = jnp.broadcast_to(seg_ref[0], (step_ref.shape[0], length))
    headcol = headcol_ref[...]
    biased, dt, rate, cum, tail, head = head_rows(step_ref[...], seg16, headcol)
    rows_ref[0] = dt
    rows_ref[1] = cum
    rows_ref[2] = tail
    rows_ref[3] = head
    dscore_ref[...] = jnp.zeros_like(dscore_ref)
    dcross_ref[...] = jnp.zeros_like(dcross_ref)
    sums_ref[...] = jnp.zeros_like(sums_ref)

    @pl.when(item == 0)
    def _():
        gconv_ref[...] = jnp.zeros_like(gconv_ref)
        ghead_ref[...] = jnp.zeros_like(ghead_ref)

    inv_row = norm_ref[0, 0:1, :]
    pull_row = norm_ref[0, 1:2, :]

    def fold(value):
        total = value[:, :TILE]
        for start in range(TILE, length, TILE):
            total = total + value[:, start : start + TILE]
        return total

    def per_head(h, carry):
        rows = pl.ds(pl.multiple_of(h * HEADDIM, HEADDIM), HEADDIM)
        one = pl.ds(first_head + h, 1)
        x_rows = pl.ds(pl.multiple_of((heads + h) * HEADDIM, HEADDIM), HEADDIM)
        taps_all = taps_ref[rows, :]
        taps = [taps_all[:, k : k + 1] for k in range(5)]
        gain = taps_all[:, 5:6]
        skip = skip_ref[2, first_head + h]
        z = z_ref[rows, :]
        y = y_ref[rows, :]
        d_o = do_ref[rows, :]
        sig_z = sigmoid(z)
        silu_z = z * sig_z
        v = y * silu_z
        dor = d_o * inv_row
        gconv_ref[5, rows, :] += fold(dor * v)
        d_v = dor * gain - v * pull_row
        dzx_ref[rows, :] = (d_v * y * (sig_z * (1.0 + z * (1.0 - sig_z)))).astype(bf16)
        dy = d_v * silu_z
        raw = raw_ref[rows, :]
        pre, shifted = conv_of(raw, taps, masks)
        sig_p = sigmoid(pre)
        xc = pre * sig_p
        dt_row = rows_ref[0, one, :]
        cum_row = rows_ref[1, one, :]
        xbar = xc * dt_row
        sums_ref[0, one, :] = jnp.sum(dy * y, axis=0, keepdims=True)
        sums_ref[1, one, :] = jnp.sum(dy * xc, axis=0, keepdims=True)
        xh, xl = split(xbar)
        yh, yl = split(dy)
        cum_col = column_of(jnp.broadcast_to(cum_row, (8, length)))
        x3 = jnp.concatenate([xh, xl, xh], axis=0)
        y3 = jnp.concatenate([yh, yh, yl], axis=0)
        parts = []
        for block in range(2):
            base = block * SPAN
            decays = [decay_tile(cum_row, cum_col, s0, t0) for s0, t0 in tiles_of(block)]
            halves = [split(decays[i] * score_ref[block * 3 + i]) for i in range(3)]
            wh = square_of([p[0] for p in halves])
            wl = square_of([p[1] for p in halves])
            byh, byl = yh[:, base : base + SPAN], yl[:, base : base + SPAN]
            both = dot(jnp.concatenate([byh, byl], axis=0), wh, NT)
            parts.append(both[:HEADDIM] + both[HEADDIM:] + dot(byh, wl, NT))
            top = dot(x3[:, base : base + TILE], y3[:, base : base + SPAN], TN)
            low = dot(x3[:, base + TILE : base + SPAN], y3[:, base + TILE : base + SPAN], TN)
            dscore_ref[block * 3] += decays[0] * top[:, :TILE]
            dscore_ref[block * 3 + 1] += decays[1] * top[:, TILE:]
            dscore_ref[block * 3 + 2] += decays[2] * low
        tail_row = rows_ref[2, one, :SPAN]
        head_row = rows_ref[3, one, :][:, SPAN:]
        dyu = dy[:, SPAN:] * head_row
        uh, ul = split(dyu)
        both = dot(jnp.concatenate([uh, ul], axis=0), bc[STATE:, SPAN:], NT)
        dstate = both[:HEADDIM] + both[HEADDIM:]
        dsh, dsl = split(dstate)
        both = dot(jnp.concatenate([dsh, dsl], axis=0), bc[:STATE, :SPAN])
        first = parts[0] + (both[:HEADDIM] + both[HEADDIM:]) * tail_row
        sh, sl = split(state_ref[0, rows, :])
        dcross_ref[1] += dot(jnp.concatenate([sh, sh, sl], axis=0), jnp.concatenate([uh, ul, uh], axis=0), TN)
        wxh, wxl = split(xbar[:, :SPAN] * tail_row)
        dcross_ref[0] += dot(jnp.concatenate([dsh, dsh, dsl], axis=0), jnp.concatenate([wxh, wxl, wxh], axis=0), TN)
        dxbar = jnp.concatenate([first, parts[1]], axis=1)
        sums_ref[2, one, :] = jnp.sum(dxbar * xc, axis=0, keepdims=True)
        dpre = (dxbar * dt_row + skip * dy) * (sig_p * (1.0 + pre * (1.0 - sig_p)))
        gconv_ref[4, rows, :] += fold(dpre)
        gconv_ref[3, rows, :] += fold(dpre * raw)
        dx = taps[3] * dpre
        for k in range(3):
            gconv_ref[2 - k, rows, :] += fold(dpre * shifted[k])
            dx = dx + taps[2 - k] * shift_left(dpre * masks[k], k + 1)
        dzx_ref[x_rows, :] = dx.astype(bf16)
        return carry

    lax.fori_loop(0, heads, per_head, 0, unroll=2)

    row = lax.broadcasted_iota(jnp.int32, (TILE, TILE), 0)
    col = lax.broadcasted_iota(jnp.int32, (TILE, TILE), 1)
    segf = seg.astype(f32)
    for block in range(2):
        base = block * SPAN
        halves = []
        for i, (s0, t0) in enumerate(tiles_of(block)):
            ok = seg_col[s0 // TILE] == segf[:1, t0 : t0 + TILE]
            if s0 == t0:
                ok = ok & (row <= col)
            halves.append(split(jnp.where(ok, dscore_ref[block * 3 + i], 0.0)))
        dh = square_of([p[0] for p in halves])
        dl = square_of([p[1] for p in halves])
        b_part = bc[:STATE, base : base + SPAN]
        c_part = bc[STATE:, base : base + SPAN]
        d_c = dot(b_part, dh) + dot(b_part, dl)
        d_b = dot(c_part, dh, NT) + dot(c_part, dl, NT)
        if block == 0:
            d_b = d_b + dcross_ref[0]
        else:
            d_c = d_c + dcross_ref[1]
        dbc_ref[:STATE, base : base + SPAN] = d_b
        dbc_ref[STATE:, base : base + SPAN] = d_c
    skipcol = headcol[:, 2:3]
    p_y, p_x, p_b = sums_ref[0], sums_ref[1], sums_ref[2]
    d_cum = p_y - skipcol * p_x - rows_ref[0] * p_b
    d_a = segment_scan_back(d_cum, seg16, SPAN)
    d_step = (p_b + d_a * rate) * sigmoid(biased)
    dstep_ref[...] = d_step.astype(bf16)
    ghead_ref[0] += fold(d_a * rate * rows_ref[0])
    ghead_ref[1] += fold(d_step)
    ghead_ref[2] += fold(p_x)

    @pl.when(item == pl.num_programs(0) - 1)
    def _():
        for index in range(6):
            gsum_ref[:, index : index + 1] = jnp.sum(gconv_ref[index], axis=1, keepdims=True)


def run_forward(first, count, before, raw, small, step_row, bc, seg, taps, headcol, head_par):
    seqs, _, length = seg.shape
    heads = head_par.shape[1]
    inner = heads * HEADDIM
    before = [] if before is None else list(before)

    def kernel(*refs):
        forward_kernel(heads, *refs[: 7], *refs[7 + len(before) :])

    grid_spec = pl.GridSpec(
        grid=(count,),
        in_specs=[
            pl.BlockSpec((inner, length), lambda i: (0, first + i)),
            pl.BlockSpec((16, length), lambda i: (step_row // 16, first + i)),
            pl.BlockSpec((2 * STATE, length), lambda i: (0, first + i)),
            pl.BlockSpec((1, 1, length), lambda i: (first + i, 0, 0)),
            pl.BlockSpec(taps.shape, lambda i: (0, 0)),
            pl.BlockSpec(headcol.shape, lambda i: (0, 0)),
            pl.BlockSpec(memory_space=pltpu.SMEM),
        ]
        + [pl.BlockSpec(memory_space=pl.ANY)] * len(before),
        out_specs=[
            pl.BlockSpec((inner, length), lambda i: (0, first + i)),
            pl.BlockSpec((1, inner, STATE), lambda i: (first + i, 0, 0)),
        ],
        scratch_shapes=[pltpu.VMEM((6, TILE, TILE), f32), pltpu.VMEM((4, 16, length), f32)],
    )
    return pl.pallas_call(
        kernel,
        grid_spec=grid_spec,
        out_shape=[
            jax.ShapeDtypeStruct((inner, seqs * length), f32),
            jax.ShapeDtypeStruct((seqs, inner, STATE), f32),
        ],
        input_output_aliases={7 + index: index for index in range(len(before))},
        compiler_params=pltpu.CompilerParams(vmem_limit_bytes=24 * 2**20),
    )(raw, small, bc, seg, taps, headcol, head_par, *before)


def run_backward(part, parts, raw, z, y, d_o, small, step_row, bc, seg, norm_rows, state, taps, headcol, head_par):
    seqs, _, length = seg.shape
    heads = head_par.shape[1] // parts
    inner = heads * HEADDIM
    big = pl.BlockSpec((inner, length), lambda i: (part, i))
    grid_spec = pl.GridSpec(
        grid=(seqs,),
        in_specs=[
            big, big, big, big,
            pl.BlockSpec((16, length), lambda i: (step_row // 16, i)),
            pl.BlockSpec((2 * STATE, length), lambda i: (0, i)),
            pl.BlockSpec((1, 1, length), lambda i: (i, 0, 0)),
            pl.BlockSpec((1, 2, length), lambda i: (i, 0, 0)),
            pl.BlockSpec((1, inner, STATE), lambda i: (i, part, 0)),
            pl.BlockSpec((inner, taps.shape[1]), lambda i: (part, 0)),
            pl.BlockSpec(headcol.shape, lambda i: (0, 0)),
            pl.BlockSpec(memory_space=pltpu.SMEM),
        ],
        out_specs=[
            pl.BlockSpec((2 * inner, length), lambda i: (0, i)),
            pl.BlockSpec((16, length), lambda i: (0, i)),
            pl.BlockSpec((2 * STATE, length), lambda i: (0, i)),
            pl.BlockSpec((inner, 8), lambda i: (0, 0)),
            pl.BlockSpec((3, 16, TILE), lambda i: (0, 0, 0)),
        ],
        scratch_shapes=[
            pltpu.VMEM((6, TILE, TILE), f32),
            pltpu.VMEM((4, 16, length), f32),
            pltpu.VMEM((6, TILE, TILE), f32),
            pltpu.VMEM((3, 16, length), f32),
            pltpu.VMEM((2, STATE, SPAN), f32),
            pltpu.VMEM((6, inner, TILE), f32),
        ],
    )
    tok = seqs * length
    return pl.pallas_call(
        functools.partial(backward_kernel, part * heads, heads),
        grid_spec=grid_spec,
        out_shape=[
            jax.ShapeDtypeStruct((2 * inner, tok), bf16),
            jax.ShapeDtypeStruct((16, tok), bf16),
            jax.ShapeDtypeStruct((2 * STATE, tok), f32),
            jax.ShapeDtypeStruct((inner, 8), f32),
            jax.ShapeDtypeStruct((3, 16, TILE), f32),
        ],
        compiler_params=pltpu.CompilerParams(vmem_limit_bytes=32 * 2**20),
    )(raw, z, y, d_o, small, bc, seg, norm_rows, state, taps, headcol, head_par)


def gate_sums_kernel(y_ref, z_ref, do_ref, taps_ref, sums_ref):
    z = z_ref[...]
    v = y_ref[...] * (z * sigmoid(z))
    gain = taps_ref[:, 5:6]
    sums_ref[0:1, :] = jnp.sum(v * v, axis=0, keepdims=True)
    sums_ref[1:2, :] = jnp.sum(do_ref[...] * gain * v, axis=0, keepdims=True)


def run_gate_sums(y, z, d_o, taps):
    inner, tok = y.shape
    block = 2 * SPAN
    big = pl.BlockSpec((inner, block), lambda i: (0, i))
    return pl.pallas_call(
        gate_sums_kernel,
        grid=(tok // block,),
        in_specs=[big, big, big, pl.BlockSpec(taps.shape, lambda i: (0, 0))],
        out_specs=pl.BlockSpec((2, block), lambda i: (0, i)),
        out_shape=jax.ShapeDtypeStruct((2, tok), f32),
    )(y, z, d_o, taps)


def gate_out_kernel(chip_ref, y_ref, z_ref, inv_ref, taps_ref, out_ref, send_ref):
    z = z_ref[...]
    v = y_ref[...] * (z * sigmoid(z))
    out = (v * inv_ref[0:1, :] * taps_ref[:, 5:6]).astype(bf16)
    out_ref[...] = out

    @pl.when(pl.program_id(0) < pl.num_programs(0) // 2)
    def _():
        send_ref[...] = out


def run_gate_out(y, z, inv, taps, chip):
    inner, tok = y.shape
    block = 2 * SPAN
    steps = tok // block
    half = steps // 2

    def at(i, chip_ref):
        return 0, lax.rem(i + (1 - chip_ref[0]) * half, steps)

    big = pl.BlockSpec((inner, block), at)
    return pl.pallas_call(
        gate_out_kernel,
        grid_spec=pltpu.PrefetchScalarGridSpec(
            num_scalar_prefetch=1,
            grid=(steps,),
            in_specs=[
                big,
                big,
                pl.BlockSpec((1, block), at),
                pl.BlockSpec(taps.shape, lambda i, chip_ref: (0, 0)),
            ],
            out_specs=[
                big,
                pl.BlockSpec((inner, block), lambda i, chip_ref: (0, jnp.minimum(i, half - 1))),
            ],
        ),
        out_shape=[
            jax.ShapeDtypeStruct((inner, tok), bf16),
            jax.ShapeDtypeStruct((inner, tok // 2), bf16),
        ],
    )(chip.reshape(1), y, z, inv, taps)


def state_forward_kernel(raw_ref, seg_ref, taps_ref, out_ref):
    seg = jnp.broadcast_to(seg_ref[0], (8, raw_ref.shape[1]))
    taps_all = taps_ref[...]
    pre, _ = conv_of(raw_ref[...], [taps_all[:, k : k + 1] for k in range(5)], conv_masks(seg))
    out_ref[...] = (pre * sigmoid(pre)).astype(bf16)


def state_backward_kernel(raw_ref, grad_ref, seg_ref, taps_ref, out_ref, gpar_ref):
    length = raw_ref.shape[1]
    seg = jnp.broadcast_to(seg_ref[0], (8, length))
    masks = conv_masks(seg)
    taps_all = taps_ref[...]
    taps = [taps_all[:, k : k + 1] for k in range(5)]
    raw = raw_ref[...]
    pre, shifted = conv_of(raw, taps, masks)
    sig = sigmoid(pre)
    dpre = grad_ref[...] * (sig * (1.0 + pre * (1.0 - sig)))

    @pl.when(pl.program_id(0) == 0)
    def _():
        gpar_ref[...] = jnp.zeros_like(gpar_ref)

    def fold(value):
        total = value[:, :TILE]
        for start in range(TILE, length, TILE):
            total = total + value[:, start : start + TILE]
        return total

    gpar_ref[4] += fold(dpre)
    gpar_ref[3] += fold(dpre * raw)
    dx = taps[3] * dpre
    for k in range(3):
        gpar_ref[2 - k] += fold(dpre * shifted[k])
        dx = dx + taps[2 - k] * shift_left(dpre * masks[k], k + 1)
    out_ref[...] = dx.astype(bf16)


def run_state_forward(proj, row, seg, taps):
    seqs, _, length = seg.shape
    width = taps.shape[0]
    return pl.pallas_call(
        state_forward_kernel,
        grid=(seqs,),
        in_specs=[
            pl.BlockSpec((width, length), lambda i: (row // width, i)),
            pl.BlockSpec((1, 1, length), lambda i: (i, 0, 0)),
            pl.BlockSpec(taps.shape, lambda i: (0, 0)),
        ],
        out_specs=pl.BlockSpec((width, length), lambda i: (0, i)),
        out_shape=jax.ShapeDtypeStruct((width, seqs * length), bf16),
    )(proj, seg, taps)


def run_state_backward(proj, row, grad, seg, taps):
    seqs, _, length = seg.shape
    width = taps.shape[0]
    return pl.pallas_call(
        state_backward_kernel,
        grid=(seqs,),
        in_specs=[
            pl.BlockSpec((width, length), lambda i: (row // width, i)),
            pl.BlockSpec((width, length), lambda i: (0, i)),
            pl.BlockSpec((1, 1, length), lambda i: (i, 0, 0)),
            pl.BlockSpec(taps.shape, lambda i: (0, 0)),
        ],
        out_specs=[
            pl.BlockSpec((width, length), lambda i: (0, i)),
            pl.BlockSpec((5, width, TILE), lambda i: (0, 0, 0)),
        ],
        out_shape=[
            jax.ShapeDtypeStruct((width, seqs * length), bf16),
            jax.ShapeDtypeStruct((5, width, TILE), f32),
        ],
    )(proj, grad, seg, taps)


def product3(left, right):
    lh, ll = split(left)
    rh, rl = split(right)
    return dot(
        jnp.concatenate([lh, lh, ll], axis=1), jnp.concatenate([rh, rl, rh], axis=0)
    )


def gram3(value):
    high, low = split(value)
    cross = dot(high, low, TN)
    return dot(high, high, TN) + cross + cross.T


def grad_kernel(place_ref, left_ref, *refs):
    right_refs, keep_ref, send_ref, both_ref = refs[:-3], refs[-3], refs[-2], refs[-1]
    groups, rows = keep_ref.shape[:2]
    left = left_ref[...]
    at = 0
    for right_ref in right_refs:
        width = right_ref.shape[0]
        part = dot(right_ref[...], left).T
        for group in range(groups):
            for side in range(2):
                start = (2 * group + side) * rows
                both_ref[side, group, :, at : at + width] = part[start : start + rows]
        at += width
    mine = place_ref[0]
    keep_ref[...] = both_ref[mine]
    send_ref[...] = both_ref[1 - mine].astype(send_ref.dtype)


def run_grad(left, rights, narrow):
    count = lax.axis_size("dp")
    tok, features = left.shape
    rows = features // count
    lanes = 3 * TILE
    groups = lanes // (2 * rows)
    cols = sum(height for _, height, _ in rights)

    def right_spec(height, index):
        return pl.BlockSpec((height, tok), lambda i, place_ref: (index, 0))

    piece = pl.BlockSpec((groups, rows, cols), lambda i, place_ref: (i, 0, 0))
    return pl.pallas_call(
        grad_kernel,
        grid_spec=pltpu.PrefetchScalarGridSpec(
            num_scalar_prefetch=1,
            grid=(features // lanes,),
            in_specs=[pl.BlockSpec((tok, lanes), lambda i, place_ref: (0, i))]
            + [right_spec(height, index) for _, height, index in rights],
            out_specs=[piece, piece],
            scratch_shapes=[pltpu.VMEM((2, groups, rows, cols), f32)],
        ),
        out_shape=[
            jax.ShapeDtypeStruct((count // 2, rows, cols), f32),
            jax.ShapeDtypeStruct((count // 2, rows, cols), bf16 if narrow else f32),
        ],
        compiler_params=pltpu.CompilerParams(vmem_limit_bytes=24 * 2**20),
    )(lax.rem(lax.axis_index("dp"), 2).reshape(1), left, *[array for array, _, _ in rights])


def pair_kernel(place_ref, keep_ref, got_ref, *outs):
    total = keep_ref[0] + got_ref[0].astype(f32)
    for index, out_ref in enumerate(outs):

        @pl.when(pl.program_id(0) == index)
        def _(out_ref=out_ref):
            out_ref[...] = total.astype(out_ref.dtype)


def run_pair(keep, got, narrow):
    groups, rows, cols = keep.shape
    kinds = [bf16 if narrow and distance > 1 else f32 for distance in range(groups)]

    def at(i, place_ref):
        return place_ref[0] ^ i, 0, 0

    block = pl.BlockSpec((1, rows, cols), at)
    return pl.pallas_call(
        pair_kernel,
        grid_spec=pltpu.PrefetchScalarGridSpec(
            num_scalar_prefetch=1,
            grid=(groups,),
            in_specs=[block, block],
            out_specs=[pl.BlockSpec((rows, cols), lambda i, place_ref: (0, 0))] * groups,
        ),
        out_shape=[jax.ShapeDtypeStruct((rows, cols), kind) for kind in kinds],
    )((lax.axis_index("dp") // 2).reshape(1), keep, got)


def summed(part_refs, cols):
    total = part_refs[0][:, cols]
    for part_ref in part_refs[1:]:
        total = total + part_ref[:, cols].astype(f32)
    return total


def momentum_kernel(count, first, extra, *refs):
    groups = (refs[:count], refs[count : 2 * count])
    refs = refs[2 * count :]
    mom_ref = refs[0]
    outs = refs[-5:] if extra else refs[-3:]
    grad_ref, new_ref, gram_ref = outs[:3]
    left = lane_iota((HEADDIM, TILE)) < HEADDIM
    for group, part_refs in enumerate(groups):

        @pl.when((pl.program_id(0) >= first) == bool(group))
        def _(part_refs=part_refs):
            for pair in range(mom_ref.shape[2] // TILE):
                cols = slice(pair * TILE, (pair + 1) * TILE)
                grad = summed(part_refs, cols)
                new = momentum_beta * mom_ref[0, :, cols] + grad
                grad_ref[0, :, cols] = grad
                new_ref[0, :, cols] = new
                gram = gram3(new)
                gram_ref[pair] = jnp.where(left, gram[:HEADDIM], gram[HEADDIM:])

    if extra:
        grad = summed([ref for ref in refs[1 : 1 + count]], slice(0, TILE))
        outs[3][...] = grad
        outs[4][...] = momentum_beta * refs[1 + count][...] + grad


def run_momentum(groups, mom, where, before, small_mom):
    _, rows, cols = mom.shape
    width = cols // 2
    pairs = width // TILE
    steps, place = where
    first = groups[0][0].shape[1] // width
    count = len(groups[0])
    extra = small_mom is not None
    before = [] if before is None else list(before)
    at = pl.BlockSpec((1, rows, width), place)
    small = pl.BlockSpec((rows, TILE), lambda i: (0, 0))

    def part_spec(lowest, highest):
        return pl.BlockSpec((rows, width), lambda i: (0, jnp.clip(i - lowest, 0, highest)))

    in_specs = [part_spec(0, first - 1)] * count + [part_spec(first, steps - first - 1)] * count + [at]
    arrays = [*groups[0], *groups[1], mom]
    if extra:
        behind = (steps - first) * pairs
        in_specs += [pl.BlockSpec((rows, TILE), lambda i: (0, behind))] * count + [small]
        arrays += [*groups[1], small_mom]
    aliases = {len(arrays) + index: index for index in range(len(before))}
    return pl.pallas_call(
        functools.partial(momentum_kernel, count, first, extra),
        grid=(steps,),
        in_specs=in_specs + [pl.BlockSpec(memory_space=pl.ANY)] * len(before),
        out_specs=[at, at, pl.BlockSpec((pairs, HEADDIM, TILE), lambda i: (i, 0, 0))] + [small] * (2 * extra),
        out_shape=[
            jax.ShapeDtypeStruct(mom.shape, f32),
            jax.ShapeDtypeStruct(mom.shape, f32),
            jax.ShapeDtypeStruct((steps * pairs, HEADDIM, TILE), f32),
        ]
        + [jax.ShapeDtypeStruct((rows, TILE), f32)] * (2 * extra),
        input_output_aliases=aliases,
    )(*arrays, *before)


def sweep(grams, norms):
    row = lax.broadcasted_iota(jnp.int32, (TILE, TILE), 0)
    col = lax.broadcasted_iota(jnp.int32, (TILE, TILE), 1)
    eye = jnp.where(row == col, 1.0, 0.0).astype(f32)
    scales = [1.0 / (norm + 1e-07) for norm in norms]
    currents = [gram * scale * scale for gram, scale in zip(grams, scales)]
    factors = None
    for step in range(NS_STEPS):
        squares = [product3(current, current) for current in currents]
        polys = [
            ns_coeffs[0] * eye + ns_coeffs[1] * current + ns_coeffs[2] * square
            for current, square in zip(currents, squares)
        ]
        if factors is None:
            factors = polys
        else:
            factors = [product3(factor, poly) for factor, poly in zip(factors, polys)]
        if step < NS_STEPS - 1:
            halves = [product3(current, poly) for current, poly in zip(currents, polys)]
            currents = [product3(poly, half) for poly, half in zip(polys, halves)]
    return [factor * scale for factor, scale in zip(factors, scales)]


def head_factor_kernel(gram_ref, got_ref, out_ref):
    left = lane_iota((HEADDIM, TILE)) < HEADDIM
    first = lane_iota((1, TILE)) < HEADDIM
    row = lax.broadcasted_iota(jnp.int32, (TILE, TILE), 0)
    col = lax.broadcasted_iota(jnp.int32, (TILE, TILE), 1)
    grams, norms = [], []
    for pair in range(gram_ref.shape[0]):
        packed = gram_ref[pair] + got_ref[pair]
        gram = jnp.concatenate(
            [jnp.where(left, packed, 0.0), jnp.where(left, 0.0, packed)], axis=0
        )
        diag = jnp.sum(jnp.where(row == col, gram, 0.0), axis=0, keepdims=True)
        low = jnp.sum(jnp.where(first, diag, 0.0), axis=1, keepdims=True)
        high = jnp.sum(jnp.where(first, 0.0, diag), axis=1, keepdims=True)
        grams.append(gram)
        norms.append(jnp.sqrt(jnp.where(first, low, high)))
    for pair, factor in enumerate(sweep(grams, norms)):
        out_ref[pair] = factor


def full_factor_kernel(gram_ref, got_ref, out_ref):
    row = lax.broadcasted_iota(jnp.int32, (TILE, TILE), 0)
    col = lax.broadcasted_iota(jnp.int32, (TILE, TILE), 1)
    grams, norms = [], []
    for block in range(gram_ref.shape[0]):
        gram = gram_ref[block] + got_ref[block]
        diag = jnp.sum(jnp.where(row == col, gram, 0.0), axis=0, keepdims=True)
        grams.append(gram)
        norms.append(jnp.broadcast_to(jnp.sqrt(jnp.sum(diag, axis=1, keepdims=True)), (1, TILE)))
    for block, factor in enumerate(sweep(grams, norms)):
        out_ref[block] = factor


def run_factor(gram, got, kernel):
    count = gram.shape[0]
    return pl.pallas_call(kernel, out_shape=jax.ShapeDtypeStruct((count, TILE, TILE), f32))(gram, got)


def apply_kernel(weight_ref, mom_ref, factor_ref, *refs):
    out_ref = refs[-1]
    for block in range(factor_ref.shape[0]):
        cols = slice(block * TILE, (block + 1) * TILE)
        ortho = product3(mom_ref[0, :, cols], factor_ref[block])
        weight = weight_ref[0, :, cols]
        out_ref[0, :, cols] = weight - muon_rate * (
            0.2 * math.sqrt(D) * ortho + decay_rate * weight
        )


def run_apply(weight, mom, factor, where, before):
    _, rows, cols = mom.shape
    width = cols // 2
    before = [] if before is None else [before]
    at = pl.BlockSpec((1, rows, width), where[1])
    return pl.pallas_call(
        apply_kernel,
        grid=(where[0],),
        in_specs=[at, at, pl.BlockSpec((width // TILE, TILE, TILE), lambda i: (i, 0, 0))]
        + [pl.BlockSpec(memory_space=pl.ANY)] * len(before),
        out_specs=at,
        out_shape=jax.ShapeDtypeStruct(weight.shape, f32),
        input_output_aliases={3: 0} if before else {},
    )(weight, mom, factor, *before)


def small_blocks(own, near, far, across, heads):
    lanes = lane_iota(own.shape)
    both = jnp.where(lanes < HEADDIM, own, pltpu.roll(near, HEADDIM, axis=1))
    steps = None
    for index, piece in enumerate((own, near, far, across)):
        part = jnp.where((lanes >= HEADDIM) & (lanes < HEADDIM + heads), piece, 0.0)
        part = pltpu.roll(part, HEADDIM + 16 * index, axis=1)
        steps = part if steps is None else steps + part
    return both, steps


def small_gram_kernel(heads, own_ref, near_ref, far_ref, across_ref, gram_ref):
    blocks = small_blocks(own_ref[...], near_ref[...], far_ref[...], across_ref[...], heads)
    for index, block in enumerate(blocks):
        gram_ref[index] = gram3(block)


def small_apply_kernel(heads, own_ref, near_ref, far_ref, across_ref, factor_ref, weight_ref, out_ref):
    blocks = small_blocks(own_ref[...], near_ref[...], far_ref[...], across_ref[...], heads)
    both = product3(blocks[0], factor_ref[0])
    steps = pltpu.roll(product3(blocks[1], factor_ref[1]), HEADDIM, axis=1)
    ortho = jnp.where(lane_iota(both.shape) < HEADDIM, both, steps)
    weight = weight_ref[...]
    out_ref[...] = weight - muon_rate * (0.2 * math.sqrt(D) * ortho + decay_rate * weight)


def flipped(count, bits):
    return [(place, place ^ bits) for place in range(count)]


def ring_places(count):
    index = lax.axis_index("dp")
    if count != 8:
        return list(range(count)), index, lambda place: place
    here = jnp.where(lax.rem(index, 2) == 0, index // 2, 7 - index // 2)
    return [0, 2, 4, 6, 7, 5, 3, 1], here, lambda place: jnp.where(place < 4, 2 * place, 15 - 2 * place)


def place_kernel(count, halves, owner_ref, *refs):
    piece_refs, out_refs = refs[: count + halves], refs[count + halves :]
    for index in range(count):

        @pl.when(pl.program_id(0) == index)
        def _(index=index):
            piece = piece_refs[index][...]
            if halves and index == count - 1:
                piece = jnp.concatenate([piece, piece_refs[count][...]], axis=0)
            at = 0
            for out_ref in out_refs:
                width = out_ref.shape[1]
                out_ref[...] = piece[:, at : at + width]
                at += width


def ring_gather(shard, widths):
    count = lax.axis_size("dp")
    order, here, owner_at = ring_places(count)
    ahead = [(order[i], order[(i + 1) % count]) for i in range(count)]
    behind = [(b, a) for a, b in ahead]
    rows = shard.shape[0]
    halves = rows % 32 == 0
    pieces, distances = [shard], [0]
    forward = backward = shard
    for step in range(1, count // 2 + 1):
        last = step == count // 2
        if last and halves:
            forward, backward = forward[: rows // 2], backward[rows // 2 :]
        forward = lax.ppermute(forward, "dp", ahead)
        pieces.append(forward)
        distances.append(-step)
        if not last or halves:
            backward = lax.ppermute(backward, "dp", behind)
            pieces.append(backward)
            distances.append(step)
    if halves:
        distances.pop()
    owners = jnp.stack([owner_at(lax.rem(here + distance + count, count)) for distance in distances])
    return pl.pallas_call(
        functools.partial(place_kernel, count, int(halves)),
        grid_spec=pltpu.PrefetchScalarGridSpec(
            num_scalar_prefetch=1,
            grid=(count,),
            in_specs=[pl.BlockSpec(piece.shape, lambda i, owner_ref: (0, 0)) for piece in pieces],
            out_specs=[
                pl.BlockSpec((rows, width), lambda i, owner_ref: (owner_ref[i], 0))
                for width in widths
            ],
        ),
        out_shape=[jax.ShapeDtypeStruct((count * rows, width), shard.dtype) for width in widths],
        compiler_params=pltpu.CompilerParams(vmem_limit_bytes=24 * 2**20),
    )(owners.astype(jnp.int32), *pieces)


def scatter_near(left, rights, narrow):
    narrow = narrow and lax.axis_size("dp") == 8
    keep, send = run_grad(left, rights, narrow)
    return keep, lax.ppermute(send, "dp", flipped(lax.axis_size("dp"), 1))


def scatter_far(near, narrow):
    count = lax.axis_size("dp")
    parts = run_pair(*near, narrow and count == 8)
    return [parts[0]] + [
        lax.ppermute(part, "dp", flipped(count, 2 * distance))
        for distance, part in enumerate(parts)
        if distance
    ]


def reduce_all(value, axis):
    count = lax.axis_size(axis)
    bits = 1
    while bits < count:
        got = lax.ppermute(value, axis, flipped(count, bits))
        if bits * 2 == count:
            return value, got
        value = value + got
        bits *= 2


def reduce_mp(value):
    near, far, across = [lax.ppermute(value, "mp", flipped(4, bits)) for bits in (1, 2, 3)]
    return (value + near) + (far + across)


def gather_mp_stack(value):
    place = lax.axis_index("mp")
    out = jnp.zeros((4,) + value.shape, value.dtype)
    out = lax.dynamic_update_index_in_dim(out, value, place, 0)
    for bits in (1, 2, 3):
        got = lax.ppermute(value, "mp", flipped(4, bits))
        out = lax.dynamic_update_index_in_dim(out, got, place ^ bits, 0)
    return out


def mp_places():
    place = lax.axis_index("mp")
    return lax.rem(place, 2), place // 2


def own_rows(value):
    core, chip = mp_places()
    quarter = value.shape[0] // 4
    return lax.dynamic_slice_in_dim(value, (chip * 2 + core) * quarter, quarter, 0)


def assemble_kernel(count, adding, place_ref, *refs):
    add_ref, out_ref = refs[0], refs[-1]
    for index, piece_ref in enumerate(refs[adding : adding + count]):

        @pl.when(pl.program_id(0) == index)
        def _(piece_ref=piece_ref):
            if adding:
                out_ref[...] = add_ref[...].astype(f32) + piece_ref[...].astype(f32)
            else:
                out_ref[...] = piece_ref[...]


def assemble(pieces, places, add, total, before):
    rows = pieces[0].shape[0]
    piece = pl.BlockSpec((rows, D), lambda i, place_ref: (0, 0))
    whole = pl.BlockSpec((rows, D), lambda i, place_ref: (place_ref[i], 0))
    adds = [] if add is None else [add]
    befores = [] if before is None else [before]
    return pl.pallas_call(
        functools.partial(assemble_kernel, len(pieces), len(adds)),
        grid_spec=pltpu.PrefetchScalarGridSpec(
            num_scalar_prefetch=1,
            grid=(len(pieces),),
            in_specs=[whole] * len(adds)
            + [piece] * len(pieces)
            + [pl.BlockSpec(memory_space=pl.ANY)] * len(befores),
            out_specs=whole,
        ),
        out_shape=jax.ShapeDtypeStruct((total, D), bf16 if add is None else f32),
        input_output_aliases={1 + len(adds) + len(pieces): 0} if befores else {},
    )(places.astype(jnp.int32), *adds, *pieces, *befores)


def norm_back_kernel(place_ref, own_ref, got_ref, x_ref, gain_ref, out_ref, ggain_ref):
    x = x_ref[...].astype(f32)
    grad = own_ref[...] + got_ref[...].astype(f32)
    inv = lax.rsqrt(jnp.mean(x * x, axis=1, keepdims=True) + eps_norm)
    scaled = grad * gain_ref[...]
    pull = jnp.mean(x * scaled, axis=1, keepdims=True)
    out_ref[...] = (scaled * inv - x * (inv * inv * inv * pull)).astype(bf16)
    ggain_ref[...] = jnp.sum(grad * (x * inv), axis=0, keepdims=True)


def run_norm_back(part, own, got, block_in, gain, quarter):
    rows = got.shape[0]
    steps = own.shape[0] // rows
    gain_spec = pl.BlockSpec((1, D), lambda i, place_ref: (0, 0))
    return pl.pallas_call(
        norm_back_kernel,
        grid_spec=pltpu.PrefetchScalarGridSpec(
            num_scalar_prefetch=1,
            grid=(1,),
            in_specs=[
                pl.BlockSpec((rows, D), lambda i, place_ref: (part, 0)),
                pl.BlockSpec((rows, D), lambda i, place_ref: (0, 0)),
                pl.BlockSpec((rows, D), lambda i, place_ref: (place_ref[0] * steps + part, 0)),
                gain_spec,
            ],
            out_specs=[pl.BlockSpec((rows, D), lambda i, place_ref: (0, 0)), gain_spec],
        ),
        out_shape=[jax.ShapeDtypeStruct((rows, D), bf16), jax.ShapeDtypeStruct((1, D), f32)],
    )(quarter.reshape(1), own, got, block_in, gain)


def input_norm(features, gain_row):
    return (
        features
        * lax.rsqrt(jnp.mean(features * features, axis=1, keepdims=True) + eps_norm)
        * gain_row
    )


def adam_update(params_in, gradient, state_pair):
    moment_one = adam_first * state_pair[0] + (1.0 - adam_first) * gradient
    moment_two = adam_second * state_pair[1] + (1.0 - adam_second) * gradient * gradient
    scaled = (
        moment_one
        / (1.0 - adam_first**adam_steps)
        / (jnp.sqrt(moment_two / (1.0 - adam_second**adam_steps)) + 1e-08)
    )
    return (params_in - adam_rate * scaled, jnp.stack([moment_one, moment_two]))


def back_normed_kernel(sel_ref, a_ref, b_ref, small_ref, wz_ref, wx_ref, ws_ref, *refs):
    wa_ref, wb_ref = refs[-2:]
    half = wz_ref.shape[1] // 2
    step = pl.program_id(0)

    @pl.when(step == 0)
    def _():
        wa_ref[:, :half] = wz_ref[:, :half]
        wa_ref[:, half:] = wx_ref[:, :half]
        wb_ref[:, :half] = wz_ref[:, half:]
        wb_ref[:, half:] = wx_ref[:, half:]

    dims = (((0,), (1,)), ((), ()))
    total = (
        dot(a_ref[...], wa_ref[...], dims)
        + dot(b_ref[...], wb_ref[...], dims)
        + dot(small_ref[...], ws_ref[...], dims)
    )
    if len(refs) == 3:
        refs[0][...] = total
    else:
        got_ref, own_ref = refs[:2]
        total = total + got_ref[...]
        for index, send_ref in enumerate(refs[2:-2]):

            @pl.when(step == index)
            def _(send_ref=send_ref):
                send_ref[...] = total.astype(bf16)

        @pl.when(step >= len(refs) - 4)
        def _():
            own_ref[...] = total


def run_back_normed(core, chip, grads, weights, got):
    tok = grads[0].shape[1]
    block = SPAN
    steps = tok // 4 // block

    def grad_at(i, sel_ref):
        here = i // steps
        quarter = jnp.where(here == 0, 1 - sel_ref[1], sel_ref[1])
        return 0, (2 * quarter + sel_ref[0]) * steps + i % steps

    in_specs = [pl.BlockSpec((grad.shape[0], block), grad_at) for grad in grads]
    in_specs += [pl.BlockSpec(weight.shape, lambda i, sel_ref: (0, 0)) for weight in weights]
    arrays = [*grads, *weights]
    if got is None:
        out_specs = pl.BlockSpec((block, D), lambda i, sel_ref: (i, 0))
        out_shape = jax.ShapeDtypeStruct((2 * steps * block, D), f32)
    else:
        in_specs.append(pl.BlockSpec((block, D), lambda i, sel_ref: (i, 0)))
        arrays.append(got)
        out_specs = [pl.BlockSpec((block, D), lambda i, sel_ref: (jnp.maximum(i - steps, 0), 0))]
        out_specs += [pl.BlockSpec((block, D), lambda i, sel_ref: (0, 0))] * steps
        out_shape = [jax.ShapeDtypeStruct((steps * block, D), f32)]
        out_shape += [jax.ShapeDtypeStruct((block, D), bf16)] * steps
    return pl.pallas_call(
        back_normed_kernel,
        grid_spec=pltpu.PrefetchScalarGridSpec(
            num_scalar_prefetch=1,
            grid=(2 * steps,),
            in_specs=in_specs,
            out_specs=out_specs,
            scratch_shapes=[pltpu.VMEM(weights[0].shape, bf16)] * 2,
        ),
        out_shape=out_shape,
        compiler_params=pltpu.CompilerParams(vmem_limit_bytes=36 * 2**20),
    )(jnp.stack([core, chip]), *arrays)


def mm(left, right, left_dim, right_dim):
    return lax.dot_general(
        left, right, (((left_dim,), (right_dim,)), ((), ())), preferred_element_type=f32
    )


def tie(*values):
    return lax.optimization_barrier(values)


def step(
    block_in,
    cotangent,
    segment_ids,
    w_heads,
    w_bc,
    w_dt,
    mom_heads,
    mom_bc,
    mom_dt,
    norm_gain,
    inner_params,
    bc_params,
    head_params,
    norm_adam,
    inner_adam,
    bc_adam,
    head_adam,
):
    seq_here, length = segment_ids.shape
    tok_rows = seq_here * length
    rows_here, inner = w_heads.shape[1:]
    heads = head_params.shape[1]
    state_cols = w_bc.shape[1]
    step_row = state_cols
    pad_steps = jnp.zeros((rows_here, TILE - state_cols - heads), bf16)
    w_x_shard = jnp.concatenate(
        [w_heads[1].astype(bf16), w_bc.astype(bf16), w_dt.astype(bf16), pad_steps], axis=1
    )
    w_x, w_s = ring_gather(w_x_shard, (inner, TILE))
    w_oz_shard = jnp.concatenate([w_heads[2].astype(bf16), w_heads[0].astype(bf16)], axis=1)
    w_o, w_z = ring_gather(w_oz_shard, (inner, inner))
    normed = input_norm(block_in.astype(f32), norm_gain).astype(bf16)
    w_heads, mom_heads, w_bc, w_dt, mom_bc, mom_dt, norm_adam, inner_adam, bc_adam, head_adam, w_s = tie(
        w_heads, mom_heads, w_bc, w_dt, mom_bc, mom_dt, norm_adam, inner_adam, bc_adam, head_adam, w_s
    )
    core, chip = mp_places()
    seg = segment_ids[:, None]
    taps = jnp.pad(inner_params.T, ((0, 0), (0, 2)))
    state_taps = jnp.pad(bc_params.T, ((0, 0), (0, 3)))
    headcol = jnp.pad(head_params.T, ((0, 16 - heads), (0, TILE - 3)))

    small = mm(w_s, normed, 0, 1)
    state_own = run_state_forward(small, 0, seg, state_taps)
    bc = gather_mp_stack(state_own).reshape(4 * state_cols, tok_rows)
    raw = mm(w_x, normed, 0, 1)
    done = None
    for first, count in ((0, 1), (1, seq_here - 2), (seq_here - 1, 1)):
        done = run_forward(
            first, count, done, raw, small, step_row, bc, seg, taps, headcol, head_params
        )
    y, state = done
    d_o = mm(w_o, cotangent, 0, 1)
    z = mm(w_z, normed, 0, 1)
    sums = run_gate_sums(y, z, d_o, taps)
    sums = reduce_mp(sums)
    sums, w_o_swap = tie(sums, w_o)
    w_o_far = lax.ppermute(w_o_swap, "mp", flipped(4, 2))
    inv = lax.rsqrt(sums[0] / INNER + eps_norm)
    pull = inv * inv * inv * sums[1] / INNER
    norm_rows = jnp.stack([inv.reshape(seq_here, length), pull.reshape(seq_here, length)], axis=1)
    out_bf, out_send = run_gate_out(y, z, inv[None], taps, chip)
    out_far = lax.ppermute(out_send, "mp", flipped(4, 2))
    o_near = scatter_near(cotangent, [(out_bf, inner, 0)], True)

    def backward(part, raw):
        return run_backward(
            part, 2, raw, z, y, d_o, small, step_row, bc, seg, norm_rows, state, taps, headcol, head_params
        )

    d_zx_a, d_step_a, d_bc_a, g_conv_a, g_head_a = backward(0, raw)
    d_zx_a, raw = tie(d_zx_a, raw)
    d_zx_b, d_step_b, d_bc_b, g_conv_b, g_head_b = backward(1, raw)
    a_near = scatter_near(normed, [(d_zx_a, inner, 0)], False)
    o_parts = scatter_far(o_near, False)
    a_parts = scatter_far(a_near, True)

    w_heads, mom_heads, d_zx_b, out_bf, block_late, cot_late = tie(
        w_heads, mom_heads, d_zx_b, out_bf, block_in, cotangent
    )
    half_tok = tok_rows // 2
    out_keep = lax.dynamic_slice_in_dim(out_bf, chip * half_tok, half_tok, 1)
    branch = mm(out_keep, w_o, 0, 1) + mm(out_far, w_o_far, 0, 1)
    branch = branch.reshape(2, half_tok // 2, D)
    send = lax.dynamic_index_in_dim(branch, 1 - core, 0, keepdims=False)
    keep = lax.dynamic_index_in_dim(branch, core, 0, keepdims=False)
    branch_own = keep + lax.ppermute(send, "mp", flipped(4, 1))
    block_own = (own_rows(block_late).astype(f32) + branch_own).astype(bf16)
    out_x = lax.ppermute(block_own, "mp", flipped(4, 2))
    out_core = lax.ppermute(block_own, "mp", flipped(4, 1))
    out_last = lax.ppermute(out_x, "mp", flipped(4, 1))
    places = jnp.stack([chip * 2 + core, chip * 2 + 1 - core, 2 - chip * 2 + core, 3 - chip * 2 - core])
    block_out = assemble([block_own, out_core, out_x, out_last], places, None, tok_rows, None)

    d_bc = (d_bc_a + d_bc_b).reshape(2, 2, state_cols, tok_rows)
    send = lax.dynamic_index_in_dim(d_bc, 1 - core, 1, keepdims=False)
    keep = lax.dynamic_index_in_dim(d_bc, core, 1, keepdims=False)
    d_bc = keep + lax.ppermute(send, "mp", flipped(4, 1))
    send = lax.dynamic_index_in_dim(d_bc, 1 - chip, 0, keepdims=False)
    keep = lax.dynamic_index_in_dim(d_bc, chip, 0, keepdims=False)
    d_state = keep + lax.ppermute(send, "mp", flipped(4, 2))
    d_raw, g_state = run_state_backward(small, 0, d_state, seg, state_taps)
    d_small = jnp.concatenate(
        [
            d_raw,
            d_step_a[: heads // 2],
            d_step_b[heads // 2 : heads],
            jnp.zeros((TILE - state_cols - heads, tok_rows), bf16),
        ],
        axis=0,
    )
    half_in = inner // 2
    c_near = scatter_near(normed, [(d_zx_b, half_in, 0)], True)
    d_near = scatter_near(normed, [(d_zx_b, half_in, 1), (d_small, TILE, 0)], False)
    c_parts = scatter_far(c_near, False)
    d_parts = scatter_far(d_near, True)

    back = (d_zx_a, d_zx_b, d_small), (w_z, w_x, w_s)
    send = run_back_normed(1 - core, chip, *back, None)
    got = lax.ppermute(send, "mp", flipped(4, 1))
    normed_own, *sends = run_back_normed(core, chip, *back, got)
    pieces = ([], [], [], [])
    gains = []
    for part, send in enumerate(sends):
        got = lax.ppermute(send, "mp", flipped(4, 2))
        back_x, gain = run_norm_back(
            part, normed_own, got, block_late, norm_gain[None], chip * 2 + core
        )
        gains.append(gain)
        far = lax.ppermute(back_x, "mp", flipped(4, 2))
        pieces[0].append(back_x)
        pieces[1].append(lax.ppermute(back_x, "mp", flipped(4, 1)))
        pieces[2].append(far)
        pieces[3].append(lax.ppermute(far, "mp", flipped(4, 1)))
    places = (places[:, None] * len(sends) + jnp.arange(len(sends))).reshape(-1)
    near_count = 2 * len(sends)
    grad_block = assemble(pieces[0] + pieces[1], places[:near_count], cot_late, tok_rows, None)
    grad_block = assemble(
        pieces[2] + pieces[3], places[near_count:], cot_late, tok_rows, grad_block
    )
    gain = sum(gains[1:], gains[0]).reshape(-1, TILE)
    gain = reduce_mp(gain)

    spots = (
        (4, lambda i: (jnp.where(i < 2, 2, i - 2), 0, jnp.where(i < 2, i, 0))),
        (2, lambda i: (i, 0, 1)),
    )
    pad_small = jnp.zeros((rows_here, TILE - state_cols - heads), f32)
    small_mom = jnp.concatenate([mom_bc, mom_dt, pad_small], axis=1)
    small_weight = jnp.concatenate([w_bc, w_dt, pad_small], axis=1)
    *stacks, gram_a = run_momentum((o_parts, a_parts), mom_heads, spots[0], None, None)
    grad_heads, new_mom_heads, gram_d, grad_small, new_small = run_momentum(
        (c_parts, d_parts), mom_heads, spots[1], stacks, small_mom
    )
    new_w_heads = None
    for gram, spot in ((gram_a, spots[0]), (gram_d, spots[1])):
        gram = reduce_all(gram, "dp")
        factor = run_factor(*gram, head_factor_kernel)
        new_w_heads = run_apply(w_heads, new_mom_heads, factor, spot, new_w_heads)
    grad_bc = grad_small[:, :state_cols]
    grad_dt = grad_small[:, state_cols : state_cols + heads]
    new_mom_bc = new_small[:, :state_cols]
    new_mom_dt = new_small[:, state_cols : state_cols + heads]
    columns = [new_small]
    for bits in (1, 2, 3):
        columns.append(lax.ppermute(new_small, "mp", flipped(4, bits)))
    gram = pl.pallas_call(
        functools.partial(small_gram_kernel, heads),
        out_shape=jax.ShapeDtypeStruct((2, TILE, TILE), f32),
    )(*columns)

    g_head = g_head_a + g_head_b
    vectors = [
        jnp.concatenate([g_conv_a, g_conv_b], axis=0),
        jnp.sum(g_state, axis=-1),
        jnp.sum(g_head, axis=-1),
        gain,
    ]
    flat = jnp.concatenate([part.reshape(-1) for part in vectors])
    sized = -(-flat.shape[0] // (8 * TILE)) * 8 * TILE
    flat = jnp.pad(flat, (0, sized - flat.shape[0])).reshape(-1, TILE)
    flat = jnp.concatenate([gram.reshape(-1, TILE), flat], axis=0)
    flat = reduce_all(flat, "dp")
    split_at = 2 * TILE
    grams = [part[:split_at].reshape(2, TILE, TILE) for part in flat]
    flat = (flat[0][split_at:] + flat[1][split_at:]).reshape(-1)
    parts = []
    at = 0
    for part in vectors:
        parts.append(flat[at : at + part.size].reshape(part.shape))
        at += part.size
    grad_inner = parts[0].T[: CONV + 2]
    grad_bc_params = parts[1]
    grad_head_params = parts[2][:, :heads]
    grad_norm_gain = parts[3].reshape(-1)
    factor = run_factor(*grams, full_factor_kernel)
    new_weight = pl.pallas_call(
        functools.partial(small_apply_kernel, heads),
        out_shape=jax.ShapeDtypeStruct((rows_here, TILE), f32),
    )(*columns, factor, small_weight)
    new_w_bc = new_weight[:, :state_cols]
    new_w_dt = new_weight[:, state_cols : state_cols + heads]
    new_norm_gain, new_norm_adam = adam_update(norm_gain, grad_norm_gain, norm_adam)
    new_inner_params, new_inner_adam = adam_update(inner_params, grad_inner, inner_adam)
    new_bc_params, new_bc_adam = adam_update(bc_params, grad_bc_params, bc_adam)
    new_head_params, new_head_adam = adam_update(head_params, grad_head_params, head_adam)
    return (
        block_out,
        grad_block,
        grad_heads,
        grad_bc,
        grad_dt,
        grad_norm_gain,
        grad_inner,
        grad_bc_params,
        grad_head_params,
        new_w_heads,
        new_w_bc,
        new_w_dt,
        new_mom_heads,
        new_mom_bc,
        new_mom_dt,
        new_norm_gain,
        new_inner_params,
        new_bc_params,
        new_head_params,
        new_norm_adam,
        new_inner_adam,
        new_bc_adam,
        new_head_adam,
    )


def solution(mesh):
    in_specs = (
        P("dp", None),
        P("dp", None),
        P("dp", None),
        P(None, "dp", "mp"),
        P("dp", "mp"),
        P("dp", "mp"),
        P(None, "dp", "mp"),
        P("dp", "mp"),
        P("dp", "mp"),
        P(),
        P(None, "mp"),
        P(None, "mp"),
        P(None, "mp"),
        P(),
        P(None, None, "mp"),
        P(None, None, "mp"),
        P(None, None, "mp"),
    )
    out_specs = (
        P("dp", None),
        P("dp", None),
        P(None, "dp", "mp"),
        P("dp", "mp"),
        P("dp", "mp"),
        P(),
        P(None, "mp"),
        P(None, "mp"),
        P(None, "mp"),
        P(None, "dp", "mp"),
        P("dp", "mp"),
        P("dp", "mp"),
        P(None, "dp", "mp"),
        P("dp", "mp"),
        P("dp", "mp"),
        P(),
        P(None, "mp"),
        P(None, "mp"),
        P(None, "mp"),
        P(),
        P(None, None, "mp"),
        P(None, None, "mp"),
        P(None, None, "mp"),
    )
    return jax.shard_map(step, mesh=mesh, in_specs=in_specs, out_specs=out_specs, check_vma=False)
```
